32 devices in a mesh: group: 2 (over x), blk: 16 (over z, y, core).
Axes of the slice: x: 2, y: 2, z: 4, core: 2. Of those that a mesh axis runs over, the one named last changes fastest.
Arguments:
- head_rows: bfloat16 [16384, 512], P(('group', 'blk')), may hold values from -1.5 to 1.5
- tail_rows: bfloat16 [16384, 512], P(('group', 'blk')), may hold values from -1.5 to 1.5
- labels: int32 [3, 16384, 64], P(None, ('group', 'blk')), may hold values from 0 to 255
- relations: bfloat16 [2, 512, 512], replicated, may hold values from -0.0390625 to 0.0390625
- hot_ids: int32 [3], replicated, may hold values from 0 to 1
- row_order: int32 [1024], replicated, may hold values from 0 to 1023, each once
- master: float32 [1024, 512], P(('group', 'blk')), may hold values from -0.25 to 0.25
- grad_squares: float32 [1024, 512], P(('group', 'blk')), may hold values from 2516 to 251658
Outputs:
- new_master: float32 [1024, 512], P(('group', 'blk'))
- transformed: bfloat16 [16384, 512], P(('group', 'blk'))
The draws below stay inside these ranges and needn't reach their ends.
Inputs may be any that keep to these rules, and one draw needn't show every extreme that they name: `hot_ids`: relation ids of the cycle steps; they may repeat. A permutation: stored row j of master and grad_squares holds row row_order[j] of the relation table. Each word packs eight 0/1 labels, bit k for tail column 8 * w + k.
All inputs are finite; a program needn't handle non-finite values.
Results may differ from the reference program's by a relative error of at most 0.0062.
Values may be sent and summed in bfloat16 or wider, within the bound.
A program may use at most 64 MiB of HBM per device.

```python
import math
import jax
import jax.numpy as jnp
from jax import lax

D = 512
HEAD_DEV = 512
TAIL_DEV = 512
RELS = 2
STEPS = 3
HEADS = 16384
TAILS = 16384
N_GROUP = 2
N_BLK = 16


def set_ends(values, own_key, least, high):
    longest = values.shape.index(max(values.shape))
    spots = []
    for shift in (0, 1):
        where = [jax.random.randint(jax.random.fold_in(own_key, axis), (), 0, length) for axis, length in enumerate(values.shape)]
        where[longest] = (where[longest] + shift) % values.shape[longest]
        spots.append(tuple(where))
    return values.at[spots[0]].set(least).at[spots[1]].set(high)


def with_spikes(values, key, source, target, shards_of, factor):
    def block_of(axis_at):
        return (jnp.arange(values.shape[axis_at]) // (values.shape[axis_at] // shards_of)).reshape((-1,) + (1,) * (values.ndim - 1 - axis_at))

    near = jax.random.permutation(key, shards_of)[block_of(target)]
    second = (block_of(target) + shards_of // 2) % shards_of
    return jnp.where((block_of(source) == near) | (block_of(source) == second), factor * values, values)


def shard_levels(own_key, shape, split, low, largest):
    loudness, own = 1.0, jax.random.fold_in(own_key, 6)
    for axis_at, blocks in split:
        steps = jnp.exp(jax.random.uniform(jax.random.fold_in(own, axis_at), (blocks,), jnp.float32, low / len(split), largest / len(split)))
        loudness = loudness * jnp.repeat(steps, shape[axis_at] // blocks).reshape([-1 if axis == axis_at else 1 for axis in range(len(shape))])
    return loudness


def gaussian(stream_key, dims, width, bound, shards=(), kind=jnp.bfloat16):
    array = width * jax.random.normal(stream_key, dims, jnp.float32)
    if shards:
        array = array * shard_levels(stream_key, dims, shards, -0.22, 0.18)
    return jnp.clip(array, -bound, bound).astype(kind)


def gaussian_with(stream_key, shape, deviation, limit, cuts, heavy, kind=jnp.bfloat16):
    drawn = deviation * jax.random.normal(stream_key, shape, jnp.float32)
    if cuts:
        drawn = drawn * shard_levels(stream_key, shape, cuts, -0.22, 0.18)
    return jnp.clip(with_spikes(drawn, jax.random.fold_in(stream_key, 3), *heavy), -limit, limit).astype(kind)


def setup_inputs(seed: int = 0) -> dict:
    key_list = jax.random.split(jax.random.key(seed), 9)
    head_rows = gaussian_with(key_list[0], (HEADS, D), 0.25, 1.5, ((0, 32),), (0, 1, 32, 2.75))
    tail_rows = gaussian(key_list[1], (TAILS, D), 0.25, 1.5, ((0, 32),))
    labels = set_ends(jax.random.randint(key_list[2], (STEPS, HEADS, TAIL_DEV // 8), 0, 256), jax.random.fold_in(key_list[2], 1), 0, 255).astype(jnp.int32)
    relations = gaussian(key_list[3], (RELS, D, D), (HEADS * TAIL_DEV * STEPS // 1024) ** -0.5, 0.0390625)
    hot_ids = jax.random.randint(key_list[4], (STEPS,), 0, RELS).astype(jnp.int32)
    row_order = jax.random.permutation(key_list[5], RELS * D).astype(jnp.int32)
    master = gaussian(key_list[6], (RELS * D, D), D ** -0.5, 0.25, ((0, 32),), jnp.float32)
    grad_squares = jnp.clip(jnp.exp(math.log(251658.0) - 4.6054007 * jax.random.uniform(key_list[7], (RELS * D, D), jnp.float32) ** shard_levels(key_list[7], (RELS * D, D), ((0, 32),), -0.2, 0.2)), 2516.0, 251658.0)
    return dict(head_rows=head_rows, tail_rows=tail_rows, labels=labels, relations=relations, hot_ids=hot_ids, row_order=row_order, master=master, grad_squares=grad_squares)


learn_rate = 0.2
tiny_floor = 1e-10

def contract_rows(left, right):
    return lax.dot_general(left, right, (((0,), (0,)), ((), ())), preferred_element_type=jnp.float32)

def contract_cols(left, right):
    return lax.dot_general(left, right, (((1,), (1,)), ((), ())), preferred_element_type=jnp.float32)

def unpack_bits(words):
    shifts = jnp.arange(8, dtype=jnp.int32)
    bits = jnp.bitwise_and(jnp.right_shift(words[:, :, None], shifts[None, None, :]), 1)
    return bits.reshape(words.shape[0], words.shape[1] * 8)

def step_gradient(head_block, tail_block, label_words, operator):
    projected = contract_cols(operator, tail_block).astype(jnp.bfloat16)
    scores = jnp.dot(head_block, projected, preferred_element_type=jnp.float32)
    targets = unpack_bits(label_words).astype(jnp.float32)
    residual = (jax.nn.sigmoid(scores) - targets).astype(jnp.bfloat16)
    partial_sum = contract_rows(head_block, residual).astype(jnp.bfloat16)
    return jnp.dot(partial_sum, tail_block, preferred_element_type=jnp.float32)

def reference(head_rows, tail_rows, labels, relations, hot_ids, row_order, master, grad_squares):
    devices = N_GROUP * N_BLK

    def one_device(gradient, device):
        head_block = lax.dynamic_slice_in_dim(head_rows, device * HEAD_DEV, HEAD_DEV, 0)
        for cycle_step in range(STEPS):
            source = device // N_BLK * N_BLK + (device % N_BLK - cycle_step) % N_BLK
            tail_block = lax.dynamic_slice_in_dim(tail_rows, source * TAIL_DEV, TAIL_DEV, 0)
            label_block = lax.dynamic_slice_in_dim(labels[cycle_step], device * HEAD_DEV, HEAD_DEV, 0)
            relation_id = hot_ids[cycle_step]
            step_term = step_gradient(head_block, tail_block, label_block, relations[relation_id])
            gradient = gradient.at[relation_id].add(step_term)
        return (gradient, None)
    gradient, unused = lax.scan(one_device, jnp.zeros((RELS, D, D), jnp.float32), jnp.arange(devices, dtype=jnp.int32))
    table_rows = RELS * D
    stored = jnp.take(gradient.reshape(table_rows, D), row_order, axis=0)
    squares_new = grad_squares + stored * stored
    new_master = master - learn_rate * stored / (jnp.sqrt(squares_new) + tiny_floor)
    positions = jnp.zeros((table_rows,), jnp.int32).at[row_order].set(jnp.arange(table_rows, dtype=jnp.int32))
    chosen = lax.dynamic_slice_in_dim(positions, hot_ids[STEPS - 1] * D, D, 0)
    operator = jnp.take(new_master.astype(jnp.bfloat16), chosen, axis=0)
    transformed = jnp.dot(head_rows, operator, preferred_element_type=jnp.float32).astype(jnp.bfloat16)
    return (new_master, transformed)
```

```python
import functools

import jax
import jax.numpy as jnp
from jax import lax
from jax.experimental import pallas as pl
from jax.experimental.pallas import tpu as pltpu
from jax.sharding import PartitionSpec as P

learn_rate = 0.2
tiny_floor = 1e-10
CHUNKS = 4


def from_behind(block, axis, distance):
    devices = range(lax.axis_size(axis))
    route = [((i - distance) % len(devices), i) for i in devices]
    return lax.ppermute(block, axis, route)


def contract_rows(left, right):
    return lax.dot_general(
        left, right, (((0,), (0,)), ((), ())), preferred_element_type=jnp.float32
    )


def contract_cols(left, right):
    return lax.dot_general(
        left, right, (((1,), (1,)), ((), ())), preferred_element_type=jnp.float32
    )


def unpack_bits(words):
    shifts = jnp.arange(8, dtype=jnp.int32)
    bits = jnp.bitwise_and(jnp.right_shift(words[:, :, None], shifts[None, None, :]), 1)
    return bits.reshape(words.shape[0], words.shape[1] * 8)


def step_gradient(head_block, tail_block, label_words, operator):
    projected = contract_cols(operator, tail_block).astype(jnp.bfloat16)
    scores = jnp.dot(head_block, projected, preferred_element_type=jnp.float32)
    targets = unpack_bits(label_words).astype(jnp.float32)
    residual = (jax.nn.sigmoid(scores) - targets).astype(jnp.bfloat16)
    partial_sum = contract_rows(head_block, residual).astype(jnp.bfloat16)
    return jnp.dot(partial_sum, tail_block, preferred_element_type=jnp.float32)


def on_device(head_rows, tail_rows, labels, relations, hot_ids, row_order, master, grad_squares):
    rel_count = relations.shape[0]
    model_width = relations.shape[1]
    step_count = labels.shape[0]
    gradient = jnp.zeros((rel_count, model_width, model_width), jnp.float32)
    tail_block = tail_rows
    for cycle_step in range(step_count):
        if cycle_step > 0:
            tail_block = from_behind(tail_block, "blk", 1)
        relation_id = hot_ids[cycle_step]
        step_term = step_gradient(head_rows, tail_block, labels[cycle_step], relations[relation_id])
        gradient = gradient.at[relation_id].add(step_term)
    table_rows = rel_count * model_width
    flat_gradient = gradient.reshape(table_rows, model_width)
    groups = lax.axis_size("group")
    blocks = lax.axis_size("blk")
    slot_rows = row_order.reshape(groups, blocks, -1).transpose(1, 0, 2).reshape(-1)
    first_sum = lax.psum_scatter(
        jnp.take(flat_gradient, slot_rows, axis=0), "blk", scatter_dimension=0, tiled=True
    )
    owned_sum = lax.psum_scatter(first_sum, "group", scatter_dimension=0, tiled=True)
    squares_new = grad_squares + owned_sum * owned_sum
    new_master = master - learn_rate * owned_sum / (jnp.sqrt(squares_new) + tiny_floor)
    updated = new_master.astype(jnp.bfloat16)
    group_rows = lax.all_gather(updated, "group", axis=0, tiled=True)
    gathered = lax.all_gather(group_rows, "blk", axis=0, tiled=True)
    positions = (
        jnp.zeros((table_rows,), jnp.int32)
        .at[slot_rows]
        .set(jnp.arange(table_rows, dtype=jnp.int32))
    )
    chosen = lax.dynamic_slice_in_dim(
        positions, hot_ids[step_count - 1] * model_width, model_width, 0
    )
    operator = jnp.take(gathered, chosen, axis=0)
    transformed = jnp.dot(head_rows, operator, preferred_element_type=jnp.float32).astype(
        jnp.bfloat16
    )
    return (new_master, transformed)


MESH = pl.DeviceIdType.MESH


def fused_body(
    dims, hot, order, head, tail, labels, relations, master, squares,
    new_master, transformed,
    tails, head_t, pick, head_pick, partials, own, core_in, pair_sum, group_in,
    group_sum, rest_in, table, send_sems, recv_sems, tail_send, tail_recv,
):
    groups, rest, rows, chunks, width = dims
    blocks = 2 * rest
    step_count, model_width = labels.shape[0], head.shape[1]
    rel_count = relations.shape[0]
    total_rows = order.shape[1]
    g = lax.axis_index("group")
    b = lax.axis_index("blk")
    core = lax.rem(b, 2)
    q = b // 2
    partner = (g, q * 2 + 1 - core)
    group_peers = [(lax.rem(g + d, groups), b) for d in range(1, groups)]
    rest_peers = [(g, lax.rem(q + d, rest) * 2 + core) for d in range(1, rest)]
    right = (g, lax.rem(b + 1, blocks))
    left = (g, lax.rem(b + blocks - 1, blocks))

    barrier = pltpu.get_barrier_semaphore()
    greeted = [partner] + group_peers + rest_peers + [right, left]
    for peer in greeted:
        pl.semaphore_signal(barrier, inc=1, device_id=peer, device_id_type=MESH)
    pl.semaphore_wait(barrier, len(greeted))

    def send(source, target, index, peer):
        copy = pltpu.make_async_remote_copy(
            src_ref=source, dst_ref=target, send_sem=send_sems.at[index],
            recv_sem=recv_sems.at[index], device_id=peer, device_id_type=MESH,
        )
        copy.start()
        return copy

    def send_tail(step):
        copy = pltpu.make_async_remote_copy(
            src_ref=tail if step == 0 else tails.at[step - 1], dst_ref=tails.at[step],
            send_sem=tail_send.at[step], recv_sem=tail_recv.at[step],
            device_id=right, device_id_type=MESH,
        )
        copy.start()
        return copy

    def tail_of(step):
        return tail if step == 0 else tails.at[step - 1]

    f32, bf16 = jnp.float32, jnp.bfloat16
    word_count = labels.shape[2]
    tail_count = word_count * 8

    def step_partial(step):
        relation = relations[hot[step]]
        projected = lax.dot_general(
            relation, tail_of(step)[...], (((1,), (1,)), ((), ())), preferred_element_type=f32
        ).astype(bf16)
        scores = jnp.dot(head[...], projected, preferred_element_type=f32)
        lane = lax.broadcasted_iota(jnp.int32, (word_count, tail_count), 1)
        word = lax.broadcasted_iota(jnp.int32, (word_count, tail_count), 0)
        spread = (lane // 8 == word).astype(f32).astype(bf16)
        words = jnp.dot(
            labels[step].astype(f32).astype(bf16), spread, preferred_element_type=f32
        ).astype(jnp.int32)
        bit = lax.broadcasted_iota(jnp.int32, words.shape, 1) % 8
        targets = ((words >> bit) & 1).astype(f32)
        residual = (jax.nn.sigmoid(scores) - targets).astype(bf16)
        partials[step] = jnp.dot(head_t[...], residual, preferred_element_type=f32).astype(bf16)

    hops = [send_tail(0)]
    head_t[...] = head[...].T
    step_partial(0)
    for step in range(1, step_count):
        hops[step - 1].wait_recv()
        if step < step_count - 1:
            hops.append(send_tail(step))
        if step == 1:
            table_index = lax.broadcasted_iota(jnp.int32, (model_width, total_rows), 0)
            last = hot[step_count - 1] * model_width
            chosen = (order[...] - last == table_index).astype(f32).astype(bf16)
            head_pick[...] = jnp.dot(head[...], chosen, preferred_element_type=f32).astype(bf16)
            spread_order = jnp.broadcast_to(order[...].astype(f32), (128, total_rows)).T
            for j in range(0, total_rows, 128):
                ids = lax.broadcasted_iota(jnp.int32, (total_rows, 128), 1).astype(f32) + j
                pick[:, j : j + 128] = (spread_order == ids).astype(f32).astype(bf16)
        step_partial(step)

    core_copies = [None] * chunks
    group_copies = [None] * chunks
    rest_copies = [None] * chunks
    back_rest = [None] * chunks
    back_group = [None] * chunks
    back_core = [None] * chunks

    def begin(k):
        cols = slice(k * width, (k + 1) * width)
        terms = [
            jnp.dot(partials[s], tail_of(s)[:, cols], preferred_element_type=f32)
            for s in range(step_count)
        ]
        gradient = []
        for r in range(rel_count):
            summed = jnp.zeros((model_width, width), f32)
            for s in range(step_count):
                summed = summed + (hot[s] == r).astype(f32) * terms[s]
            gradient.append(summed.astype(bf16))
        stored = jnp.dot(
            pick[...], jnp.concatenate(gradient, axis=0), preferred_element_type=f32
        ).astype(bf16)
        own[k] = stored.reshape(2, groups, rest, rows, width)
        core_copies[k] = [send(own.at[k, 1 - core], core_in.at[k], (k, 0), partner)]

    def over_group(k):
        for copy in core_copies[k]:
            copy.wait_recv()
        pair_sum[k] = (own[k, core].astype(f32) + core_in[k].astype(f32)).astype(bf16)
        group_copies[k] = [
            send(pair_sum.at[k, peer[0]], group_in.at[k, d], (k, 1 + d), peer)
            for d, peer in enumerate(group_peers)
        ]

    def over_rest(k):
        for copy in group_copies[k]:
            copy.wait_recv()
        summed = own[k, core, g].astype(f32) + core_in[k, g].astype(f32)
        for d in range(groups - 1):
            summed = summed + group_in[k, d].astype(f32)
        group_sum[k] = summed.astype(bf16)
        rest_copies[k] = [
            send(
                group_sum.at[k, lax.rem(q + d + 1, rest)], rest_in.at[k, d],
                (k, groups + d), peer,
            )
            for d, peer in enumerate(rest_peers)
        ]

    def update(k):
        cols = slice(k * width, (k + 1) * width)
        for copy in rest_copies[k]:
            copy.wait_recv()
        summed = group_sum[k, q].astype(f32)
        for d in range(rest - 1):
            summed = summed + rest_in[k, d].astype(f32)
        squares_new = squares[:, cols] + summed * summed
        updated = master[:, cols] - learn_rate * summed / (jnp.sqrt(squares_new) + tiny_floor)
        new_master[:, cols] = updated
        table[k, core, g, q] = updated.astype(bf16)
        mine = table.at[k, core, g, q]
        back_rest[k] = [
            send(mine, mine, (k, groups + rest - 1 + d), peer)
            for d, peer in enumerate(rest_peers)
        ]

    def gather_group(k):
        for copy in back_rest[k]:
            copy.wait_recv()
        mine = table.at[k, core, g]
        back_group[k] = [
            send(mine, mine, (k, groups + 2 * (rest - 1) + d), peer)
            for d, peer in enumerate(group_peers)
        ]

    def gather_core(k):
        for copy in back_group[k]:
            copy.wait_recv()
        mine = table.at[k, core]
        back_core[k] = [send(mine, mine, (k, 2 * (groups + rest - 2) + 1), partner)]

    def finish(k):
        cols = slice(k * width, (k + 1) * width)
        for copy in back_core[k]:
            copy.wait_recv()
        operator = table[k].reshape(total_rows, width)
        transformed[:, cols] = jnp.dot(
            head_pick[...], operator, preferred_element_type=f32
        ).astype(bf16)

    stages = [begin, over_group, over_rest, update, gather_group, gather_core, finish]
    for t in range(chunks + len(stages) - 1):
        for k in range(chunks):
            if 0 <= t - k < len(stages):
                stages[t - k](k)

    for copy in hops:
        copy.wait_send()
    for k in range(chunks):
        for lot in (core_copies, group_copies, rest_copies, back_rest, back_group, back_core):
            for copy in lot[k]:
                copy.wait_send()


def on_device_fused(head_rows, tail_rows, labels, relations, hot_ids, row_order, master, grad_squares):
    groups = lax.axis_size("group")
    rest = lax.axis_size("blk") // 2
    rows, model_width = master.shape
    steps = labels.shape[0]
    heads = head_rows.shape[0]
    table_rows = relations.shape[0] * model_width
    chunks = CHUNKS
    width = model_width // chunks
    order = row_order.reshape(groups, rest, 2, rows).transpose(2, 0, 1, 3).reshape(1, -1)
    copies = 2 * (groups + rest - 2) + 2
    bf16 = jnp.bfloat16
    vmem = pl.BlockSpec(memory_space=pltpu.VMEM)
    smem = pl.BlockSpec(memory_space=pltpu.SMEM)
    return tuple(pl.pallas_call(
        functools.partial(fused_body, (groups, rest, rows, chunks, width)),
        out_shape=(
            jax.ShapeDtypeStruct(master.shape, jnp.float32),
            jax.ShapeDtypeStruct((heads, model_width), bf16),
        ),
        in_specs=[smem] + [vmem] * 7,
        out_specs=(vmem, vmem),
        scratch_shapes=[
            pltpu.VMEM((steps - 1,) + tail_rows.shape, bf16),
            pltpu.VMEM((model_width, heads), bf16),
            pltpu.VMEM((table_rows, table_rows), bf16),
            pltpu.VMEM((heads, table_rows), bf16),
            pltpu.VMEM((steps, model_width, tail_rows.shape[0]), bf16),
            pltpu.VMEM((chunks, 2, groups, rest, rows, width), bf16),
            pltpu.VMEM((chunks, groups, rest, rows, width), bf16),
            pltpu.VMEM((chunks, groups, rest, rows, width), bf16),
            pltpu.VMEM((chunks, groups - 1, rest, rows, width), bf16),
            pltpu.VMEM((chunks, rest, rows, width), bf16),
            pltpu.VMEM((chunks, rest - 1, rows, width), bf16),
            pltpu.VMEM((chunks, 2, groups, rest, rows, width), bf16),
            pltpu.SemaphoreType.DMA((chunks, copies)),
            pltpu.SemaphoreType.DMA((chunks, copies)),
            pltpu.SemaphoreType.DMA((steps - 1,)),
            pltpu.SemaphoreType.DMA((steps - 1,)),
        ],
        compiler_params=pltpu.CompilerParams(
            collective_id=0, has_side_effects=True, vmem_limit_bytes=60000 * 1024
        ),
        name="rescal_update",
    )(hot_ids, order, head_rows, tail_rows, labels, relations, master, grad_squares))


def fits_fused(mesh, args):
    groups, blocks = mesh.shape["group"], mesh.shape["blk"]
    rows = args[6].shape[0] // (groups * blocks)
    steps = args[2].shape[0]
    return rows % 16 == 0 and blocks % 2 == 0 and blocks > 2 and groups > 1 and steps > 1


def solution(mesh):
    in_specs = (
        P(("group", "blk"), None),
        P(("group", "blk"), None),
        P(None, ("group", "blk"), None),
        P(),
        P(),
        P(),
        P(("group", "blk"), None),
        P(("group", "blk"), None),
    )
    out_specs = (P(("group", "blk"), None), P(("group", "blk"), None))
    def run(*args):
        body = on_device_fused if fits_fused(mesh, args) else on_device
        return jax.shard_map(
            body, mesh=mesh, in_specs=in_specs, out_specs=out_specs, check_vma=False
        )(*args)

    return run
```

```python
import functools

import jax
import jax.numpy as jnp
from jax import lax
from jax.experimental import pallas as pl
from jax.experimental.pallas import tpu as pltpu
from jax.sharding import PartitionSpec as P

learn_rate = 0.2
tiny_floor = 1e-10
CHUNKS = 4
PAIR = 2
SCHEDULE = [("b", 0), ("b", 2)] + [(stage, k) for stage in "gruG" for k in range(CHUNKS)] + [
    ("C", 0), ("C", 1), ("f", 0), ("C", 2), ("C", 3), ("f", 2),
]


def from_behind(block, axis, distance):
    devices = range(lax.axis_size(axis))
    route = [((i - distance) % len(devices), i) for i in devices]
    return lax.ppermute(block, axis, route)


def contract_rows(left, right):
    return lax.dot_general(
        left, right, (((0,), (0,)), ((), ())), preferred_element_type=jnp.float32
    )


def contract_cols(left, right):
    return lax.dot_general(
        left, right, (((1,), (1,)), ((), ())), preferred_element_type=jnp.float32
    )


def unpack_bits(words):
    shifts = jnp.arange(8, dtype=jnp.int32)
    bits = jnp.bitwise_and(jnp.right_shift(words[:, :, None], shifts[None, None, :]), 1)
    return bits.reshape(words.shape[0], words.shape[1] * 8)


def step_gradient(head_block, tail_block, label_words, operator):
    projected = contract_cols(operator, tail_block).astype(jnp.bfloat16)
    scores = jnp.dot(head_block, projected, preferred_element_type=jnp.float32)
    targets = unpack_bits(label_words).astype(jnp.float32)
    residual = (jax.nn.sigmoid(scores) - targets).astype(jnp.bfloat16)
    partial_sum = contract_rows(head_block, residual).astype(jnp.bfloat16)
    return jnp.dot(partial_sum, tail_block, preferred_element_type=jnp.float32)


def on_device(head_rows, tail_rows, labels, relations, hot_ids, row_order, master, grad_squares):
    rel_count = relations.shape[0]
    model_width = relations.shape[1]
    step_count = labels.shape[0]
    gradient = jnp.zeros((rel_count, model_width, model_width), jnp.float32)
    tail_block = tail_rows
    for cycle_step in range(step_count):
        if cycle_step > 0:
            tail_block = from_behind(tail_block, "blk", 1)
        relation_id = hot_ids[cycle_step]
        step_term = step_gradient(head_rows, tail_block, labels[cycle_step], relations[relation_id])
        gradient = gradient.at[relation_id].add(step_term)
    table_rows = rel_count * model_width
    flat_gradient = gradient.reshape(table_rows, model_width)
    groups = lax.axis_size("group")
    blocks = lax.axis_size("blk")
    slot_rows = row_order.reshape(groups, blocks, -1).transpose(1, 0, 2).reshape(-1)
    first_sum = lax.psum_scatter(
        jnp.take(flat_gradient, slot_rows, axis=0), "blk", scatter_dimension=0, tiled=True
    )
    owned_sum = lax.psum_scatter(first_sum, "group", scatter_dimension=0, tiled=True)
    squares_new = grad_squares + owned_sum * owned_sum
    new_master = master - learn_rate * owned_sum / (jnp.sqrt(squares_new) + tiny_floor)
    updated = new_master.astype(jnp.bfloat16)
    group_rows = lax.all_gather(updated, "group", axis=0, tiled=True)
    gathered = lax.all_gather(group_rows, "blk", axis=0, tiled=True)
    positions = (
        jnp.zeros((table_rows,), jnp.int32)
        .at[slot_rows]
        .set(jnp.arange(table_rows, dtype=jnp.int32))
    )
    chosen = lax.dynamic_slice_in_dim(
        positions, hot_ids[step_count - 1] * model_width, model_width, 0
    )
    operator = jnp.take(gathered, chosen, axis=0)
    transformed = jnp.dot(head_rows, operator, preferred_element_type=jnp.float32).astype(
        jnp.bfloat16
    )
    return (new_master, transformed)


MESH = pl.DeviceIdType.MESH


def fused_body(
    dims, hot, order, head_src, tail_src, labels_src, relations_src, master_src, squares_src,
    new_master, transformed,
    head, tail, labels, relations, master, squares, tails, head_t, pick, head_pick, partials, own, core_in, pair_sum, group_in,
    group_sum, rest_in, table, send_sems, recv_sems, tail_send, tail_recv, load_sems,
):
    groups, rest, rows, chunks, width = dims
    blocks = 2 * rest
    step_count, model_width = labels.shape[0], head.shape[1]
    rel_count = relations.shape[0]
    total_rows = order.shape[1]
    g = lax.axis_index("group")
    b = lax.axis_index("blk")
    core = lax.rem(b, 2)
    q = b // 2
    partner = (g, q * 2 + 1 - core)
    group_peers = [(lax.rem(g + d, groups), b) for d in range(1, groups)]
    rest_peers = [(g, lax.rem(q + d, rest) * 2 + core) for d in range(1, rest)]
    right = (g, lax.rem(b + 1, blocks))
    left = (g, lax.rem(b + blocks - 1, blocks))

    sources = (head_src, relations_src, tail_src, labels_src, master_src, squares_src)
    targets = (head, relations, tail, labels, master, squares)
    loads = [
        pltpu.make_async_copy(source, target, load_sems.at[i])
        for i, (source, target) in enumerate(zip(sources, targets))
    ]
    for load in loads:
        load.start()

    barrier = pltpu.get_barrier_semaphore()
    greeted = [partner] + group_peers + rest_peers + [right, left]
    for peer in greeted:
        pl.semaphore_signal(barrier, inc=1, device_id=peer, device_id_type=MESH)
    pl.semaphore_wait(barrier, len(greeted))

    def send(source, target, index, peer):
        copy = pltpu.make_async_remote_copy(
            src_ref=source, dst_ref=target, send_sem=send_sems.at[index],
            recv_sem=recv_sems.at[index], device_id=peer, device_id_type=MESH,
        )
        copy.start()
        return copy

    def send_tail(step):
        copy = pltpu.make_async_remote_copy(
            src_ref=tail_src if step == 0 else tails.at[step - 1], dst_ref=tails.at[step],
            send_sem=tail_send.at[step], recv_sem=tail_recv.at[step],
            device_id=right, device_id_type=MESH,
        )
        copy.start()
        return copy

    def tail_of(step):
        return tail if step == 0 else tails.at[step - 1]

    f32, bf16 = jnp.float32, jnp.bfloat16
    word_count = labels.shape[1]
    tail_count = word_count * 8

    def step_partial(step):
        relation = relations[hot[step]]
        projected = lax.dot_general(
            relation, tail_of(step)[...], (((1,), (1,)), ((), ())), preferred_element_type=f32
        ).astype(bf16)
        scores = jnp.dot(head[...], projected, preferred_element_type=f32)
        lane = lax.broadcasted_iota(jnp.int32, (word_count, tail_count), 1)
        word = lax.broadcasted_iota(jnp.int32, (word_count, tail_count), 0)
        spread = (lane // 8 == word).astype(f32).astype(bf16)
        words = contract_rows(labels[step].astype(f32).astype(bf16), spread).astype(jnp.int32)
        bit = lax.broadcasted_iota(jnp.int32, words.shape, 1) % 8
        targets = ((words >> bit) & 1).astype(f32)
        residual = (jax.nn.sigmoid(scores) - targets).astype(bf16)
        partials[step] = jnp.dot(head_t[...], residual, preferred_element_type=f32).astype(bf16)

    hops = [send_tail(0)]
    for load in loads:
        load.wait()
    head_t[...] = head[...].T
    step_partial(0)
    for step in range(1, step_count):
        hops[step - 1].wait_recv()
        if step < step_count - 1:
            hops.append(send_tail(step))
        if step == 1:
            table_index = lax.broadcasted_iota(jnp.int32, (model_width, total_rows), 0)
            last = hot[step_count - 1] * model_width
            chosen = (order[...] - last == table_index).astype(f32).astype(bf16)
            head_pick[...] = jnp.dot(head[...], chosen, preferred_element_type=f32).astype(bf16)
            spread_order = jnp.broadcast_to(order[...].astype(f32), (128, total_rows)).T
            for j in range(0, total_rows, 128):
                ids = lax.broadcasted_iota(jnp.int32, (total_rows, 128), 1).astype(f32) + j
                pick[:, j : j + 128] = (spread_order == ids).astype(f32).astype(bf16)
        step_partial(step)

    core_copies = [None] * chunks
    group_copies = [None] * chunks
    rest_copies = [None] * chunks
    back_rest = [None] * chunks
    back_group = [None] * chunks
    back_core = [None] * chunks

    def begin(k):
        cols = slice(k * width, (k + PAIR) * width)
        terms = [
            jnp.dot(partials[s], tail_of(s)[:, cols], preferred_element_type=f32)
            for s in range(step_count)
        ]
        gradient = []
        for r in range(rel_count):
            summed = jnp.zeros((model_width, PAIR * width), f32)
            for s in range(step_count):
                summed = summed + (hot[s] == r).astype(f32) * terms[s]
            gradient.append(summed.astype(bf16))
        stored = jnp.dot(
            pick[...], jnp.concatenate(gradient, axis=0), preferred_element_type=f32
        ).astype(bf16)
        for i in range(k, k + PAIR):
            part = stored[:, (i - k) * width : (i - k + 1) * width]
            own[i] = part.reshape(groups, rest, 2, rows, width)
            core_copies[i] = [send(own.at[i, :, :, 1 - core], core_in.at[i], (i, 0), partner)]

    def over_group(k):
        for copy in core_copies[k]:
            copy.wait_recv()
        pair_sum[k] = (own[k, :, :, core].astype(f32) + core_in[k].astype(f32)).astype(bf16)
        group_copies[k] = [
            send(pair_sum.at[k, peer[0]], group_in.at[k, d], (k, 1 + d), peer)
            for d, peer in enumerate(group_peers)
        ]

    def over_rest(k):
        for copy in group_copies[k]:
            copy.wait_recv()
        summed = own[k, g, :, core].astype(f32) + core_in[k, g].astype(f32)
        for d in range(groups - 1):
            summed = summed + group_in[k, d].astype(f32)
        group_sum[k] = summed.astype(bf16)
        rest_copies[k] = [
            send(
                group_sum.at[k, lax.rem(q + d + 1, rest)], rest_in.at[k, d],
                (k, groups + d), peer,
            )
            for d, peer in enumerate(rest_peers)
        ]

    def update(k):
        cols = slice(k * width, (k + 1) * width)
        for copy in rest_copies[k]:
            copy.wait_recv()
        summed = group_sum[k, q].astype(f32)
        for d in range(rest - 1):
            summed = summed + rest_in[k, d].astype(f32)
        squares_new = squares[:, cols] + summed * summed
        updated = master[:, cols] - learn_rate * summed / (jnp.sqrt(squares_new) + tiny_floor)
        new_master[:, cols] = updated
        table[k, g, q, core] = updated.astype(bf16)
        mine = table.at[k, g, q, core]
        back_rest[k] = [
            send(mine, mine, (k, groups + rest - 1 + d), peer)
            for d, peer in enumerate(rest_peers)
        ]

    def gather_group(k):
        for copy in back_rest[k]:
            copy.wait_recv()
        mine = table.at[k, g, :, core]
        back_group[k] = [
            send(mine, mine, (k, groups + 2 * (rest - 1) + d), peer)
            for d, peer in enumerate(group_peers)
        ]

    def gather_core(k):
        for copy in back_group[k]:
            copy.wait_recv()
        mine = table.at[k, :, :, core]
        back_core[k] = [send(mine, mine, (k, 2 * (groups + rest - 2) + 1), partner)]

    def finish(k):
        cols = slice(k * width, (k + PAIR) * width)
        for i in range(k, k + PAIR):
            for copy in back_core[i]:
                copy.wait_recv()
        operator = jnp.concatenate(
            [table[i].reshape(total_rows, width) for i in range(k, k + PAIR)], axis=1
        )
        transformed[:, cols] = jnp.dot(
            head_pick[...], operator, preferred_element_type=f32
        ).astype(bf16)

    stages = dict(
        b=begin, g=over_group, r=over_rest, u=update, G=gather_group, C=gather_core, f=finish
    )
    for stage, k in SCHEDULE:
        stages[stage](k)

    for copy in hops:
        copy.wait_send()
    for k in range(chunks):
        for lot in (core_copies, group_copies, rest_copies, back_rest, back_group, back_core):
            for copy in lot[k]:
                copy.wait_send()


def on_device_fused(head_rows, tail_rows, labels, relations, hot_ids, row_order, master, grad_squares):
    groups = lax.axis_size("group")
    rest = lax.axis_size("blk") // 2
    rows, model_width = master.shape
    steps = labels.shape[0]
    heads = head_rows.shape[0]
    table_rows = relations.shape[0] * model_width
    chunks = CHUNKS
    width = model_width // chunks
    order = row_order.reshape(1, -1)
    copies = 2 * (groups + rest - 2) + 2
    bf16 = jnp.bfloat16
    vmem = pl.BlockSpec(memory_space=pltpu.VMEM)
    smem = pl.BlockSpec(memory_space=pltpu.SMEM)
    hbm = pl.BlockSpec(memory_space=pltpu.HBM)
    words = labels.transpose(0, 2, 1)
    results = pl.pallas_call(
        functools.partial(fused_body, (groups, rest, rows, chunks, width)),
        out_shape=(
            jax.ShapeDtypeStruct(master.shape, jnp.float32),
            jax.ShapeDtypeStruct((heads, model_width), bf16),
        ),
        in_specs=[smem, vmem] + [hbm] * 6,
        out_specs=(vmem, vmem),
        scratch_shapes=[
            pltpu.VMEM(x.shape, x.dtype)
            for x in (head_rows, tail_rows, words, relations, master, grad_squares)
        ] + [
            pltpu.VMEM((steps - 1,) + tail_rows.shape, bf16),
            pltpu.VMEM((model_width, heads), bf16),
            pltpu.VMEM((table_rows, table_rows), bf16),
            pltpu.VMEM((heads, table_rows), bf16),
            pltpu.VMEM((steps, model_width, tail_rows.shape[0]), bf16),
            pltpu.VMEM((chunks, groups, rest, 2, rows, width), bf16),
            pltpu.VMEM((chunks, groups, rest, rows, width), bf16),
            pltpu.VMEM((chunks, groups, rest, rows, width), bf16),
            pltpu.VMEM((chunks, groups - 1, rest, rows, width), bf16),
            pltpu.VMEM((chunks, rest, rows, width), bf16),
            pltpu.VMEM((chunks, rest - 1, rows, width), bf16),
            pltpu.VMEM((chunks, groups, rest, 2, rows, width), bf16),
            pltpu.SemaphoreType.DMA((chunks, copies)),
            pltpu.SemaphoreType.DMA((chunks, copies)),
            pltpu.SemaphoreType.DMA((steps - 1,)),
            pltpu.SemaphoreType.DMA((steps - 1,)),
            pltpu.SemaphoreType.DMA((6,)),
        ],
        compiler_params=pltpu.CompilerParams(
            collective_id=0, has_side_effects=True, vmem_limit_bytes=60000 * 1024
        ),
        name="rescal_update",
    )(hot_ids, order, head_rows, tail_rows, words, relations, master, grad_squares)
    return keep_results(results)


def keep_body(first, second, first_out, second_out):
    first_out[...] = first[...]
    second_out[...] = second[...]


def keep_results(results):
    vmem = pl.BlockSpec(memory_space=pltpu.VMEM)
    return tuple(pl.pallas_call(
        keep_body,
        out_shape=tuple(jax.ShapeDtypeStruct(r.shape, r.dtype) for r in results),
        in_specs=[vmem, vmem],
        out_specs=(vmem, vmem),
        name="keep_results",
    )(*results))


def fits_fused(mesh, args):
    groups, blocks = mesh.shape["group"], mesh.shape["blk"]
    rows = args[6].shape[0] // (groups * blocks)
    steps = args[2].shape[0]
    return rows % 16 == 0 and blocks % 2 == 0 and blocks > 2 and groups > 1 and steps > 1


def solution(mesh):
    in_specs = (
        P(("group", "blk"), None),
        P(("group", "blk"), None),
        P(None, ("group", "blk"), None),
        P(),
        P(),
        P(),
        P(("group", "blk"), None),
        P(("group", "blk"), None),
    )
    out_specs = (P(("group", "blk"), None), P(("group", "blk"), None))
    def run(*args):
        body = on_device_fused if fits_fused(mesh, args) else on_device
        return jax.shard_map(
            body, mesh=mesh, in_specs=in_specs, out_specs=out_specs, check_vma=False
        )(*args)

    return run
```
